32 devices in a mesh: dp: 8 (over z, core), tensor: 4 (over y, x).
Axes of the slice: x: 2, y: 2, z: 4, core: 2. Of those that a mesh axis runs over, the one named last changes fastest.
Arguments:
- tokens: bfloat16 [24576, 1536], P(('dp', 'tensor')), may hold values from -6 to 6
- cotangent: bfloat16 [24576, 1536], P(('dp', 'tensor')), may hold values from -6 to 6
- seg_ids: int32 [8, 3072], P('dp'), may hold values from 0 to 3, never falling along the last dimension, each value on 1 to 2048 neighbouring positions
- gain_attn: bfloat16 [1536], P('dp'), may hold values from 0.5 to 1.5
- gain_ffn: bfloat16 [1536], P('dp'), may hold values from 0.5 to 1.5
- w_query: bfloat16 [1536, 1536], P('dp', 'tensor'), may hold values from -0.17860863 to 0.17860863
- w_key: bfloat16 [1536, 768], P('dp', 'tensor'), may hold values from -0.17860863 to 0.17860863
- value_projection: bfloat16 [1536, 768], P('dp', 'tensor'), may hold values from -0.15625 to 0.15625
- w_out: bfloat16 [1536, 1536], P('tensor', 'dp'), may hold values from -0.625 to 0.625
- w_gate: bfloat16 [1536, 4096], P('dp', 'tensor'), may hold values from -0.15625 to 0.15625
- w_up: bfloat16 [1536, 4096], P('dp', 'tensor'), may hold values from -0.15625 to 0.15625
- w_down: bfloat16 [4096, 1536], P('tensor', 'dp'), may hold values from -0.09375 to 0.09375
Outputs:
- layer_out: bfloat16 [24576, 1536], P(('dp', 'tensor'))
- grad_tokens: float32 [24576, 1536], P(('dp', 'tensor'))
- grad_gain_attn: float32 [1536], P('dp')
- grad_gain_ffn: float32 [1536], P('dp')
- grad_query: float32 [1536, 1536], P('dp', 'tensor')
- grad_key: float32 [1536, 768], P('dp', 'tensor')
- grad_value: float32 [1536, 768], P('dp', 'tensor')
- grad_out: float32 [1536, 1536], P('tensor', 'dp')
- grad_gate: float32 [1536, 4096], P('dp', 'tensor')
- grad_up: float32 [1536, 4096], P('dp', 'tensor')
- grad_down: float32 [4096, 1536], P('tensor', 'dp')
The draws below stay inside these ranges and needn't reach their ends.
Inputs may be any that keep to these rules, and one draw needn't show every extreme that they name: `seg_ids`: in each pack the values never fall along the tokens; each of the 4 sequences has 1 to 2048 tokens, and one of them exactly 2048.
All inputs are finite; a program needn't handle non-finite values.
Results may differ from the reference program's by a relative error of at most 0.02.
Values may be sent and summed in bfloat16 or wider, within the bound.
No kernel may reach another device: no remote copies, remote signals or barrier semaphores. Data moves between devices by JAX's collectives and lax.ppermute only.
A program may use at most 256 MiB of HBM per device.

```python
import math
import jax
import jax.numpy as jnp
import numpy as np
from jax import lax

MODEL_WIDTH = 1536
QUERY_HEADS = 16
KEY_VALUE_HEADS = 8
HEAD_SIZE = 96
FF = 4096
TOKENS_PER_PACK = 3072
SEGS = 4
MAXLEN = 2048
TOKEN_TOTAL = 24576
N_DP = 8


def weight_base(key, columns):
    noise = jnp.clip(jax.random.normal(key, (MODEL_WIDTH, columns), jnp.float32), -6.0, 6.0)
    return noise * MODEL_WIDTH ** (-0.5)


def draw_w_query(key, part):
    weight_matrix = weight_base(jax.random.fold_in(key, 11), QUERY_HEADS * HEAD_SIZE)
    return weight_matrix.astype(jnp.bfloat16)


def draw_w_key(key, part):
    weight_matrix = weight_base(jax.random.fold_in(key, 12), KEY_VALUE_HEADS * HEAD_SIZE)
    return weight_matrix.astype(jnp.bfloat16)


def draw_tokens(key, part):
    return jnp.clip(jax.random.normal(jax.random.fold_in(key, 13), (TOKEN_TOTAL, MODEL_WIDTH), jnp.float32), -6.0, 6.0).astype(jnp.bfloat16)


def block_levels(own_key, dims, pieces, low, high):
    factor_of = 1.0
    for axis_at, shards_of in pieces:
        heights = jax.random.uniform(jax.random.fold_in(jax.random.fold_in(own_key, 6), axis_at), (shards_of,), jnp.float32, low / len(pieces), high / len(pieces))
        factor_of = factor_of * jnp.repeat(jnp.exp(heights), dims[axis_at] // shards_of).reshape((-1,) + (1,) * (len(dims) - 1 - axis_at))
    return factor_of


def length_profile(number_of, total, bound, lean):
    portions = [(1 << 20) // math.isqrt(grade ** lean) + 1 for grade in range(2, number_of + 1)]
    spare, counts = total - bound - (number_of - 1), [1] * (number_of - 1)
    while spare > 0:
        free = [i for i in range(number_of - 1) if counts[i] < bound]
        pool, budget = sum([portions[i] for i in free]), spare
        for i in free:
            addition = min(bound - counts[i], max(1, budget * portions[i] // pool), spare)
            counts[i] = counts[i] + addition
            spare = spare - addition
    return np.array([bound] + counts)


def ragged_sizes(stream_key, count, total, most, lean):
    if count == 2:
        one = jax.random.randint(stream_key, (), max(1, total - most), min(most, total - 1) + 1)
        return jnp.stack([one, total - one])
    tallies = jnp.asarray(length_profile(count, total, most, lean), jnp.int32)
    couples = (count - 1) // 2
    giver, taker = tallies[1:1 + 2 * couples:2], tallies[2:2 + 2 * couples:2]
    room = jnp.minimum(giver - 1, most - taker)
    moved = jax.random.randint(jax.random.fold_in(stream_key, 1), (couples,), 0, 1 << 20) % (room + 1)
    tallies = tallies.at[1:1 + 2 * couples:2].set(giver - moved).at[2:2 + 2 * couples:2].set(taker + moved)
    return tallies[jax.random.permutation(jax.random.fold_in(stream_key, 2), count)]


def centred(rng, extent, scale, limit, split=(), kind=jnp.bfloat16):
    drawn = jax.random.normal(rng, extent, jnp.float32) * scale
    if len(split) > 0:
        drawn = block_levels(rng, extent, split, -0.22, 0.18) * drawn
    return jnp.clip(drawn, min=-limit, max=limit).astype(kind)


def setup_inputs(seed: int = 0) -> dict:
    key_list = jax.random.split(jax.random.key(seed), 13)
    return {
        "tokens": draw_tokens(jax.random.fold_in(key_list[12], 71), 0),
        "cotangent": centred(key_list[1], (TOKEN_TOTAL, MODEL_WIDTH), 1.0, 6.0, ((0, 32),)),
        "seg_ids": jax.vmap(lambda own: jnp.searchsorted(jnp.cumsum(ragged_sizes(own, SEGS, TOKENS_PER_PACK, MAXLEN, 2)), jnp.arange(TOKENS_PER_PACK), side="right"))(jax.random.split(key_list[2], N_DP)).reshape((N_DP, TOKENS_PER_PACK)).astype(jnp.int32),
        "gain_attn": jnp.clip(1.0 + 0.1 * jax.random.normal(key_list[3], (MODEL_WIDTH,), jnp.float32), 0.5, 1.5).astype(jnp.bfloat16),
        "gain_ffn": jnp.clip(1.0 + 0.1 * jax.random.normal(key_list[4], (MODEL_WIDTH,), jnp.float32), 0.5, 1.5).astype(jnp.bfloat16),
        "w_query": draw_w_query(jax.random.fold_in(key_list[12], 71), 0),
        "w_key": draw_w_key(jax.random.fold_in(key_list[12], 71), 0),
        "value_projection": centred(key_list[7], (MODEL_WIDTH, KEY_VALUE_HEADS * HEAD_SIZE), MODEL_WIDTH ** -0.5, 0.15625, ((0, 8), (1, 4))),
        "w_out": centred(key_list[8], (QUERY_HEADS * HEAD_SIZE, MODEL_WIDTH), (QUERY_HEADS * HEAD_SIZE // 16) ** -0.5, 0.625, ((0, 4), (1, 8))),
        "w_gate": centred(key_list[9], (MODEL_WIDTH, FF), MODEL_WIDTH ** -0.5, 0.15625, ((0, 8), (1, 4))),
        "w_up": centred(key_list[10], (MODEL_WIDTH, FF), MODEL_WIDTH ** -0.5, 0.15625, ((0, 8), (1, 4))),
        "w_down": centred(key_list[11], (FF, MODEL_WIDTH), FF ** -0.5, 0.09375, ((0, 4), (1, 8))),
    }


rope_base = 100000.0
small_eps = 1e-05
masked_value = -1e+30

@jax.custom_vjp
def low(v):
    return lax.optimization_barrier(v.astype(jnp.bfloat16)).astype(jnp.float32)

@jax.custom_vjp
def lower_backward(v):
    return v

def low_keep(v):
    return (low(v), None)

def low_pass(kept, grad):
    return (grad,)

def back_keep(v):
    return (v, None)

def back_low(kept, grad):
    return (low(grad),)
low.defvjp(low_keep, low_pass)
lower_backward.defvjp(back_keep, back_low)

def matrix_product(left, right):
    return jnp.dot(left, right, precision=lax.Precision.HIGHEST, preferred_element_type=jnp.float32)

def positions(segment_ids):
    length_axis = segment_ids.shape[-1]
    labels = jnp.arange(SEGS, dtype=jnp.int32)
    member = (segment_ids[..., :, None] == labels).astype(jnp.int32)
    lengths_of = lax.optimization_barrier(jnp.sum(member, axis=-2))
    earlier = (labels < segment_ids[..., :, None]).astype(jnp.int32)
    first_row = lax.optimization_barrier(jnp.sum(earlier * lengths_of[..., None, :], axis=-1))
    return jnp.arange(length_axis, dtype=jnp.int32) - first_row

def angles_of(position_ids):
    frequency = rope_base ** (-jnp.arange(HEAD_SIZE // 2, dtype=jnp.float32) * 2.0 / HEAD_SIZE)
    phase_angle = position_ids.astype(jnp.float32)[..., None] * frequency
    return (jnp.cos(phase_angle), jnp.sin(phase_angle))

def rotate(values, cosine, sine_table):
    half_width = values.shape[-1] // 2
    front_half = values[..., :half_width]
    back_half = values[..., half_width:]
    return jnp.concatenate([front_half * cosine - back_half * sine_table, back_half * cosine + front_half * sine_table], axis=-1)

def rms_scale(hidden):
    return lax.rsqrt(lax.optimization_barrier(jnp.mean(hidden * hidden, axis=-1, keepdims=True)) + small_eps)

def attend_pack(query_rows, rows_of_keys, rows_of_values, segment_row):
    rows_of_block = min(512, TOKENS_PER_PACK)
    block_list = TOKENS_PER_PACK // rows_of_block
    score_scale = HEAD_SIZE ** (-0.5)
    blocks_of_queries = query_rows.reshape(block_list, rows_of_block, KEY_VALUE_HEADS, QUERY_HEADS // KEY_VALUE_HEADS, HEAD_SIZE)
    begins = jnp.arange(block_list, dtype=jnp.int32) * rows_of_block
    key_index = jnp.arange(TOKENS_PER_PACK, dtype=jnp.int32)

    def one_block(query_block, begin_row):
        raw_scores = jnp.einsum('qcgd,kcd->cgqk', query_block, rows_of_keys, precision=lax.Precision.HIGHEST)
        scores = lower_backward(raw_scores) * score_scale
        query_index = begin_row + jnp.arange(rows_of_block, dtype=jnp.int32)
        query_segment = lax.dynamic_slice_in_dim(segment_row, begin_row, rows_of_block)
        allowed = (query_segment[:, None] == segment_row[None, :]) & (key_index[None, :] <= query_index[:, None])
        scores = jnp.where(allowed, scores, masked_value)
        largest = lax.optimization_barrier(jnp.max(scores, axis=-1, keepdims=True))
        exp_scores = jnp.exp(scores - largest)
        softmax_rows = low(exp_scores / lax.optimization_barrier(jnp.sum(exp_scores, axis=-1, keepdims=True)))
        return jnp.einsum('cgqk,kcd->qcgd', softmax_rows, rows_of_values, precision=lax.Precision.HIGHEST)

    def mapped(block_args):
        return jax.checkpoint(one_block)(block_args[0], block_args[1])
    outputs = lax.map(mapped, (blocks_of_queries, begins))
    return outputs.reshape(TOKENS_PER_PACK, QUERY_HEADS * HEAD_SIZE)

def reference(tokens, cotangent, seg_ids, gain_attn, gain_ffn, w_query, w_key, value_projection, w_out, w_gate, w_up, w_down):
    cosine, sine_table = angles_of(positions(seg_ids))
    cosine = cosine.reshape(TOKEN_TOTAL, 1, HEAD_SIZE // 2)
    sine_table = sine_table.reshape(TOKEN_TOTAL, 1, HEAD_SIZE // 2)

    def attention(query_rows, rows_of_keys, rows_of_values):
        packed_queries = query_rows.reshape(N_DP, TOKENS_PER_PACK, KEY_VALUE_HEADS, QUERY_HEADS // KEY_VALUE_HEADS, HEAD_SIZE)
        packed_keys = rows_of_keys.reshape(N_DP, TOKENS_PER_PACK, KEY_VALUE_HEADS, HEAD_SIZE)
        packed_values = rows_of_values.reshape(N_DP, TOKENS_PER_PACK, KEY_VALUE_HEADS, HEAD_SIZE)

        def mapped(pack_args):
            return jax.checkpoint(attend_pack)(pack_args[0], pack_args[1], pack_args[2], pack_args[3])
        outputs = lax.map(mapped, (packed_queries, packed_keys, packed_values, seg_ids))
        return outputs.reshape(TOKEN_TOTAL, QUERY_HEADS * HEAD_SIZE)

    def forward(hidden, gain_one, gain_two, query_w, key_matrix, value_matrix, out_w, gate_w, up_w, down_w):
        attention_input = low(hidden * rms_scale(hidden) * gain_one)
        query_lin = lower_backward(matrix_product(attention_input, query_w)).reshape(TOKEN_TOTAL, QUERY_HEADS, HEAD_SIZE)
        key_linear = lower_backward(matrix_product(attention_input, key_matrix)).reshape(TOKEN_TOTAL, KEY_VALUE_HEADS, HEAD_SIZE)
        value_linear = lower_backward(matrix_product(attention_input, value_matrix)).reshape(TOKEN_TOTAL, KEY_VALUE_HEADS, HEAD_SIZE)
        query_rows = low(rotate(query_lin, cosine, sine_table))
        rows_of_keys = low(rotate(key_linear, cosine, sine_table))
        rows_of_values = low(value_linear)
        attn_rows = low(lower_backward(attention(query_rows, rows_of_keys, rows_of_values)))
        branch = lower_backward(matrix_product(attn_rows, out_w))
        hidden_mid = hidden + branch
        ffn_input = low(hidden_mid * rms_scale(hidden_mid) * gain_two)
        gate_lin = lower_backward(matrix_product(ffn_input, gate_w))
        up_lin = lower_backward(matrix_product(ffn_input, up_w))
        units_out = low(jax.nn.silu(gate_lin) * up_lin)
        return hidden_mid + matrix_product(units_out, down_w)
    inputs = (tokens.astype(jnp.float32), gain_attn.astype(jnp.float32), gain_ffn.astype(jnp.float32), w_query.astype(jnp.float32), w_key.astype(jnp.float32), value_projection.astype(jnp.float32), w_out.astype(jnp.float32), w_gate.astype(jnp.float32), w_up.astype(jnp.float32), w_down.astype(jnp.float32))
    result, pullback = jax.vjp(forward, inputs[0], inputs[1], inputs[2], inputs[3], inputs[4], inputs[5], inputs[6], inputs[7], inputs[8], inputs[9])
    gradients = pullback(cotangent.astype(jnp.float32))
    return (result.astype(jnp.bfloat16), gradients[0], gradients[1], gradients[2], gradients[3], gradients[4], gradients[5], gradients[6], gradients[7], gradients[8], gradients[9])
```

```python
import functools
import jax
import jax.numpy as jnp
from jax import lax
from jax.experimental import pallas as pl
from jax.experimental.pallas import tpu as pltpu
from jax.sharding import PartitionSpec as P

QUERY_HEADS = 16
KEY_VALUE_HEADS = 8
HEAD_SIZE = 96
SEGS = 4


rope_base = 100000.0
small_eps = 1e-05
masked_value = -1e30


def matrix_product(left, right):
    return jnp.dot(left, right, preferred_element_type=jnp.float32)


def dot_rows(left, right):
    return lax.dot_general(
        left, right, (((0,), (0,)), ((), ())), preferred_element_type=jnp.float32
    )


def dot_cols(left, right):
    return lax.dot_general(
        left, right, (((1,), (1,)), ((), ())), preferred_element_type=jnp.float32
    )


def positions(segment_ids):
    length_axis = segment_ids.shape[-1]
    labels = jnp.arange(SEGS, dtype=jnp.int32)
    member = (segment_ids[..., :, None] == labels).astype(jnp.int32)
    lengths_of = jnp.sum(member, axis=-2)
    earlier = (labels < segment_ids[..., :, None]).astype(jnp.int32)
    first_row = jnp.sum(earlier * lengths_of[..., None, :], axis=-1)
    return jnp.arange(length_axis, dtype=jnp.int32) - first_row


def angles_of(position_ids):
    frequency = rope_base ** (-jnp.arange(HEAD_SIZE // 2, dtype=jnp.float32) * 2.0 / HEAD_SIZE)
    phase_angle = position_ids.astype(jnp.float32)[..., None] * frequency
    return (jnp.cos(phase_angle), jnp.sin(phase_angle))


def rotate(values, cosine, sine_table):
    half_width = values.shape[-1] // 2
    front_half = values[..., :half_width]
    back_half = values[..., half_width:]
    return jnp.concatenate(
        [
            front_half * cosine - back_half * sine_table,
            back_half * cosine + front_half * sine_table,
        ],
        axis=-1,
    )


def unrotate(values, cosine, sine_table):
    half_width = values.shape[-1] // 2
    front_half = values[..., :half_width]
    back_half = values[..., half_width:]
    return jnp.concatenate(
        [
            front_half * cosine + back_half * sine_table,
            back_half * cosine - front_half * sine_table,
        ],
        axis=-1,
    )


def rms_scale(hidden):
    return lax.rsqrt(jnp.mean(hidden * hidden, axis=-1, keepdims=True) + small_eps)


def norm_back(grad_normed, normed, inverse, gain):
    scaled = grad_normed * gain
    return inverse * (scaled - normed * jnp.mean(scaled * normed, axis=-1, keepdims=True))


LOG2E = 1.4426950408889634


def dot_f32(left, right):
    return jnp.dot(left, right, preferred_element_type=jnp.float32)


def block_mask(kv_block, q_block, block, starts, diagonal):
    keys = kv_block * block + lax.broadcasted_iota(jnp.int32, (block, starts.shape[1]), 0)
    allowed = keys >= starts
    if diagonal:
        group = starts.shape[1] // block
        lanes = lax.broadcasted_iota(jnp.int32, (1, block), 1) + q_block * block
        allowed = allowed & (keys <= jnp.concatenate([lanes] * group, axis=1))
    return allowed


def forward_kernel(
    low_ref, high_ref, start_ref, qkv_ref, out_ref, lse_ref, qt_ref, k_ref, vt_ref, acc_ref,
    *, heads, kv_heads, block, scale,
):
    step = pl.program_id(0)
    rows = qkv_ref.shape[0]
    group = heads // kv_heads
    factor = scale * LOG2E
    q_width = heads * HEAD_SIZE
    k_width = kv_heads * HEAD_SIZE

    @pl.when(step == 0)
    def _():
        @pl.loop(0, rows // block)
        def _(at):
            here = pl.ds(pl.multiple_of(at * block, block), block)
            turned = qkv_ref[here, :].T
            qt_ref[:, here] = turned[:q_width]
            for kv in range(kv_heads):
                begin = q_width + kv * HEAD_SIZE
                k_ref[kv, here, :] = turned[begin : begin + HEAD_SIZE].T
                begin = begin + k_width
                vt_ref[kv, :HEAD_SIZE, here] = turned[begin : begin + HEAD_SIZE]
                vt_ref[kv, HEAD_SIZE:, here] = jnp.ones((16, block), jnp.bfloat16)

    here = pl.ds(pl.multiple_of(step * block, block), block)
    starts = jnp.concatenate([start_ref[:, here]] * group, axis=1)
    turned_queries = [
        jnp.concatenate(
            [
                qt_ref[(kv * group + g) * HEAD_SIZE : (kv * group + g + 1) * HEAD_SIZE, here]
                for g in range(group)
            ],
            axis=1,
        )
        for kv in range(kv_heads)
    ]

    def scores(kv, kv_block, masked, diagonal):
        there = pl.ds(pl.multiple_of(kv_block * block, block), block)
        raw = dot_f32(k_ref[kv, there, :], turned_queries[kv])
        if masked:
            raw = jnp.where(
                block_mask(kv_block, step, block, starts, diagonal), raw, masked_value
            )
        return raw

    def attend(kv, kv_block, probs):
        there = pl.ds(pl.multiple_of(kv_block * block, block), block)
        return dot_f32(vt_ref[kv, :, there], probs.astype(jnp.bfloat16))

    largest = []
    for kv in range(kv_heads):
        raw = scores(kv, step, True, True)
        top = jnp.max(raw, axis=0, keepdims=True)
        acc_ref[kv] = attend(kv, step, jnp.exp2((raw - top) * factor))
        largest.append(top)

    def more(masked):
        def body(kv_block, tops):
            result = []
            for kv in range(kv_heads):
                raw = scores(kv, kv_block, masked, False)
                top = jnp.maximum(tops[kv], jnp.max(raw, axis=0, keepdims=True))
                shrink = jnp.exp2((tops[kv] - top) * factor)
                acc_ref[kv] = acc_ref[kv] * shrink + attend(
                    kv, kv_block, jnp.exp2((raw - top) * factor)
                )
                result.append(top)
            return tuple(result)

        return body

    low = low_ref[step]
    high = jnp.minimum(high_ref[step], step)
    tops = lax.fori_loop(low, high, more(True), tuple(largest))
    tops = lax.fori_loop(jnp.maximum(low, high), step, more(False), tops)
    outs = []
    for kv in range(kv_heads):
        total = acc_ref[kv, HEAD_SIZE : HEAD_SIZE + 1, :]
        result = (acc_ref[kv, :HEAD_SIZE, :] / total).astype(jnp.bfloat16)
        logs = tops[kv] * factor + jnp.log2(total)
        for g in range(group):
            outs.append(result[:, g * block : (g + 1) * block])
            lse_ref[kv * group + g : kv * group + g + 1, :] = logs[:, g * block : (g + 1) * block]
    out_ref[...] = jnp.concatenate(outs, axis=0).T


def attention_forward(qkv, starts, low, high, heads, kv_heads, block):
    rows, width = qkv.shape
    q_width = heads * HEAD_SIZE
    group = heads // kv_heads
    return pl.pallas_call(
        functools.partial(
            forward_kernel, heads=heads, kv_heads=kv_heads, block=block, scale=HEAD_SIZE**-0.5
        ),
        grid_spec=pltpu.PrefetchScalarGridSpec(
            num_scalar_prefetch=2,
            grid=(rows // block,),
            in_specs=[
                pl.BlockSpec((1, rows), lambda i, *_: (0, 0)),
                pl.BlockSpec((rows, width), lambda i, *_: (0, 0)),
            ],
            out_specs=[
                pl.BlockSpec((block, q_width), lambda i, *_: (i, 0)),
                pl.BlockSpec((heads, block), lambda i, *_: (0, i)),
            ],
            scratch_shapes=[
                pltpu.VMEM((q_width, rows), jnp.bfloat16),
                pltpu.VMEM((kv_heads, rows, HEAD_SIZE), jnp.bfloat16),
                pltpu.VMEM((kv_heads, HEAD_SIZE + 16, rows), jnp.bfloat16),
                pltpu.VMEM((kv_heads, HEAD_SIZE + 16, group * block), jnp.float32),
            ],
        ),
        out_shape=[
            jax.ShapeDtypeStruct((rows, q_width), jnp.bfloat16),
            jax.ShapeDtypeStruct((heads, rows), jnp.float32),
        ],
        name="attention_forward",
    )(low, high, starts, qkv)


def unrotate_turned(values, cosine, sine_table):
    half = HEAD_SIZE // 2
    front, back = values[:half], values[half:]
    return jnp.concatenate(
        [front * cosine + back * sine_table, back * cosine - front * sine_table], axis=0
    )


def backward_kernel(
    low_ref, high_ref, start_ref, qkv_ref, out_ref, grad_ref, lse_ref, cos_ref, sin_ref,
    result_ref, k_ref, kt_ref, v_ref, dk_ref, dv_ref, dq_ref, turned_ref,
    *, heads, kv_heads, block, scale,
):
    step = pl.program_id(0)
    rows = qkv_ref.shape[0]
    group = heads // kv_heads
    factor = scale * LOG2E
    q_width = heads * HEAD_SIZE
    k_width = kv_heads * HEAD_SIZE

    @pl.when(step == 0)
    def _():
        dk_ref[...] = jnp.zeros_like(dk_ref)
        dv_ref[...] = jnp.zeros_like(dv_ref)

        @pl.loop(0, rows // block)
        def _(at):
            here = pl.ds(pl.multiple_of(at * block, block), block)
            turned = qkv_ref[here, :].T
            for kv in range(kv_heads):
                begin = q_width + kv * HEAD_SIZE
                kt_ref[kv, :, here] = turned[begin : begin + HEAD_SIZE]
                k_ref[kv, here, :] = turned[begin : begin + HEAD_SIZE].T
                begin = begin + k_width
                v_ref[kv, here, :] = turned[begin : begin + HEAD_SIZE].T

    here = pl.ds(pl.multiple_of(step * block, block), block)
    starts = jnp.concatenate([start_ref[:, here]] * group, axis=1)
    turned_q = qkv_ref[here, :].T
    turned_grad = grad_ref[...].T
    turned_out = out_ref[...].T
    product = turned_grad.astype(jnp.float32) * turned_out.astype(jnp.float32)
    queries, queries_turned, grads, grads_turned, inners, logs = [], [], [], [], [], []
    for kv in range(kv_heads):
        pieces = [
            (slice((kv * group + g) * HEAD_SIZE, (kv * group + g + 1) * HEAD_SIZE))
            for g in range(group)
        ]
        queries_turned.append(jnp.concatenate([turned_q[s] for s in pieces], axis=1))
        grads_turned.append(jnp.concatenate([turned_grad[s] for s in pieces], axis=1))
        queries.append(jnp.concatenate([turned_q[s].T for s in pieces], axis=0))
        grads.append(jnp.concatenate([turned_grad[s].T for s in pieces], axis=0))
        inners.append(
            jnp.concatenate([jnp.sum(product[s], axis=0, keepdims=True) for s in pieces], axis=1)
        )
        logs.append(
            jnp.concatenate(
                [lse_ref[kv * group + g : kv * group + g + 1, :] for g in range(group)], axis=1
            )
        )

    def block_step(kv_block, masked, diagonal):
        there = pl.ds(pl.multiple_of(kv_block * block, block), block)
        if masked:
            allowed = block_mask(kv_block, step, block, starts, diagonal)
        for kv in range(kv_heads):
            raw = dot_f32(k_ref[kv, there, :], queries_turned[kv])
            if masked:
                raw = jnp.where(allowed, raw, masked_value)
            probs = jnp.exp2(raw * factor - logs[kv])
            grad_soft = dot_f32(v_ref[kv, there, :], grads_turned[kv])
            grad_raw = (probs * (grad_soft - inners[kv])).astype(jnp.bfloat16)
            dv_ref[kv, there, :] += dot_f32(probs.astype(jnp.bfloat16), grads[kv])
            dk_ref[kv, there, :] += dot_f32(grad_raw, queries[kv])
            dq = dot_f32(kt_ref[kv, :, there], grad_raw)
            if diagonal:
                dq_ref[kv] = dq
            else:
                dq_ref[kv] += dq

    block_step(step, True, True)
    low = low_ref[step]
    high = jnp.minimum(high_ref[step], step)

    @pl.loop(low, high)
    def _(kv_block):
        block_step(kv_block, True, False)

    @pl.loop(jnp.maximum(low, high), step)
    def _(kv_block):
        block_step(kv_block, False, False)

    cosine, sine_table = cos_ref[:, here], sin_ref[:, here]
    for kv in range(kv_heads):
        for g in range(group):
            head = kv * group + g
            turned = dq_ref[kv, :, g * block : (g + 1) * block] * scale
            turned_ref[head * HEAD_SIZE : (head + 1) * HEAD_SIZE, here] = unrotate_turned(
                turned, cosine, sine_table
            ).astype(jnp.bfloat16)

    @pl.when(step == pl.num_programs(0) - 1)
    def _():
        @pl.loop(0, rows // block)
        def _(at):
            here = pl.ds(pl.multiple_of(at * block, block), block)
            pieces = [turned_ref[:, here]]
            for kv in range(kv_heads):
                turned = dk_ref[kv, here, :].T * scale
                pieces.append(
                    unrotate_turned(turned, cos_ref[:, here], sin_ref[:, here]).astype(
                        jnp.bfloat16
                    )
                )
            for kv in range(kv_heads):
                pieces.append(dv_ref[kv, here, :].T.astype(jnp.bfloat16))
            result_ref[here, :] = jnp.concatenate(pieces, axis=0).T


def attention_backward(
    qkv, out, grad, logs, starts, low, high, cosine, sine_table, heads, kv_heads, block
):
    rows, width = qkv.shape
    q_width = heads * HEAD_SIZE
    group = heads // kv_heads
    half = HEAD_SIZE // 2
    whole = lambda i, *_: (0, 0)
    return pl.pallas_call(
        functools.partial(
            backward_kernel, heads=heads, kv_heads=kv_heads, block=block, scale=HEAD_SIZE**-0.5
        ),
        grid_spec=pltpu.PrefetchScalarGridSpec(
            num_scalar_prefetch=2,
            grid=(rows // block,),
            in_specs=[
                pl.BlockSpec((1, rows), whole),
                pl.BlockSpec((rows, width), whole),
                pl.BlockSpec((block, q_width), lambda i, *_: (i, 0)),
                pl.BlockSpec((block, q_width), lambda i, *_: (i, 0)),
                pl.BlockSpec((heads, block), lambda i, *_: (0, i)),
                pl.BlockSpec((half, rows), whole),
                pl.BlockSpec((half, rows), whole),
            ],
            out_specs=pl.BlockSpec((rows, width), whole),
            scratch_shapes=[
                pltpu.VMEM((kv_heads, rows, HEAD_SIZE), jnp.bfloat16),
                pltpu.VMEM((kv_heads, HEAD_SIZE, rows), jnp.bfloat16),
                pltpu.VMEM((kv_heads, rows, HEAD_SIZE), jnp.bfloat16),
                pltpu.VMEM((kv_heads, rows, HEAD_SIZE), jnp.float32),
                pltpu.VMEM((kv_heads, rows, HEAD_SIZE), jnp.float32),
                pltpu.VMEM((kv_heads, HEAD_SIZE, group * block), jnp.float32),
                pltpu.VMEM((q_width, rows), jnp.bfloat16),
            ],
        ),
        out_shape=jax.ShapeDtypeStruct((rows, width), jnp.bfloat16),
        name="attention_backward",
    )(low, high, starts, qkv, out, grad, logs, cosine, sine_table)


def block_bounds(starts, block):
    firsts = starts[0, ::block]
    lasts = starts[0, block - 1 :: block]
    return firsts // block, (lasts + block - 1) // block


def on_device(
    tokens,
    cotangent,
    seg_ids,
    gain_attn,
    gain_ffn,
    w_query,
    w_key,
    value_projection,
    w_out,
    w_gate,
    w_up,
    w_down,
):
    gathered = (
        lax.all_gather(gain_attn, "dp", axis=0, tiled=True),
        lax.all_gather(gain_ffn, "dp", axis=0, tiled=True),
        lax.all_gather(w_query, "dp", axis=0, tiled=True),
        lax.all_gather(w_key, "dp", axis=0, tiled=True),
        lax.all_gather(value_projection, "dp", axis=0, tiled=True),
        lax.all_gather(w_out, "dp", axis=1, tiled=True),
        lax.all_gather(w_gate, "dp", axis=0, tiled=True),
        lax.all_gather(w_up, "dp", axis=0, tiled=True),
        lax.all_gather(w_down, "dp", axis=1, tiled=True),
    )
    gain_one = gathered[0].astype(jnp.float32)
    gain_two = gathered[1].astype(jnp.float32)
    query_weight, key_weight, value_weight, out_weight, gate_weight, up_weight, down_weight = (
        gathered[2:]
    )
    segment_row = seg_ids[0]
    pack_rows = segment_row.shape[0]
    kv_local = key_weight.shape[1] // HEAD_SIZE
    group_width = QUERY_HEADS // KEY_VALUE_HEADS
    heads_local = kv_local * group_width
    position_ids = positions(segment_row)
    cosine, sine_table = angles_of(position_ids)
    cosine_heads = cosine[:, None, None, :]
    sine_heads = sine_table[:, None, None, :]
    cosine_keys = cosine[:, None, :]
    sine_keys = sine_table[:, None, :]
    hidden_in = tokens.astype(jnp.float32)
    inverse_one = rms_scale(hidden_in)
    normed_one = hidden_in * inverse_one
    attention_input = (normed_one * gain_one).astype(jnp.bfloat16)
    attn_rows = lax.all_gather(attention_input, "tensor", axis=0, tiled=True)
    query_lin = matrix_product(attn_rows, query_weight).reshape(
        pack_rows, kv_local, group_width, HEAD_SIZE
    )
    query_rot = rotate(query_lin, cosine_heads, sine_heads).astype(jnp.bfloat16)
    key_linear = matrix_product(attn_rows, key_weight).reshape(pack_rows, kv_local, HEAD_SIZE)
    key_rot = rotate(key_linear, cosine_keys, sine_keys).astype(jnp.bfloat16)
    rows_of_values = (
        matrix_product(attn_rows, value_weight)
        .astype(jnp.bfloat16)
        .reshape(pack_rows, kv_local, HEAD_SIZE)
    )
    qkv = jnp.concatenate(
        [
            query_rot.reshape(pack_rows, heads_local * HEAD_SIZE),
            key_rot.reshape(pack_rows, kv_local * HEAD_SIZE),
            rows_of_values.reshape(pack_rows, kv_local * HEAD_SIZE),
        ],
        axis=1,
    )
    starts = (jnp.arange(pack_rows, dtype=jnp.int32) - position_ids)[None, :]
    low_512, high_512 = block_bounds(starts, 512)
    low_256, high_256 = block_bounds(starts, 256)
    attn_out, log_totals = attention_forward(
        qkv, starts, low_512, high_512, heads_local, kv_local, 512
    )
    branch = lax.psum_scatter(
        matrix_product(attn_out, out_weight), "tensor", scatter_dimension=0, tiled=True
    )
    hidden_mid = hidden_in + branch
    inverse_two = rms_scale(hidden_mid)
    normed_two = hidden_mid * inverse_two
    ffn_input = (normed_two * gain_two).astype(jnp.bfloat16)
    cotangent_full = cotangent.astype(jnp.float32)
    ffn_rows = lax.all_gather(ffn_input, "tensor", axis=0, tiled=True)
    gate_lin = matrix_product(ffn_rows, gate_weight)
    up_lin = matrix_product(ffn_rows, up_weight)
    gate_sigmoid = jax.nn.sigmoid(gate_lin)
    gate_act = gate_lin * gate_sigmoid
    units_out = (gate_act * up_lin).astype(jnp.bfloat16)
    result = (
        hidden_mid
        + lax.psum_scatter(
            matrix_product(units_out, down_weight).astype(jnp.bfloat16),
            "tensor",
            scatter_dimension=0,
            tiled=True,
        ).astype(jnp.float32)
    ).astype(jnp.bfloat16)
    cotangent_rows = lax.all_gather(cotangent, "tensor", axis=0, tiled=True)
    grad_units = dot_cols(cotangent_rows, down_weight)
    grad_gate_lin = (
        grad_units * up_lin * gate_sigmoid * (1.0 + gate_lin * (1.0 - gate_sigmoid))
    ).astype(jnp.bfloat16)
    grad_up_lin = (grad_units * gate_act).astype(jnp.bfloat16)
    grad_gate_w = dot_rows(ffn_rows, grad_gate_lin)
    grad_up_w = dot_rows(ffn_rows, grad_up_lin)
    grad_down_w = dot_rows(units_out, cotangent_rows)
    grad_ffn_input = lax.psum_scatter(
        dot_cols(grad_gate_lin, gate_weight) + dot_cols(grad_up_lin, up_weight),
        "tensor",
        scatter_dimension=0,
        tiled=True,
    )
    grad_mid = cotangent_full + norm_back(grad_ffn_input, normed_two, inverse_two, gain_two)
    gain_two_part = jnp.sum(grad_ffn_input * normed_two, axis=0)
    grad_branch = grad_mid.astype(jnp.bfloat16)
    branch_rows = lax.all_gather(grad_branch, "tensor", axis=0, tiled=True)
    grad_out_w = dot_rows(attn_out, branch_rows)
    grad_attended = dot_cols(branch_rows, out_weight).astype(jnp.bfloat16)
    grad_qkv = attention_backward(
        qkv,
        attn_out,
        grad_attended,
        log_totals,
        starts,
        low_256,
        high_256,
        cosine.T,
        sine_table.T,
        heads_local,
        kv_local,
        256,
    )
    query_grad, key_grad_low, value_grad_low = jnp.split(
        grad_qkv,
        [heads_local * HEAD_SIZE, (heads_local + kv_local) * HEAD_SIZE],
        axis=1,
    )
    grad_query_w = dot_rows(attn_rows, query_grad)
    grad_key_w = dot_rows(attn_rows, key_grad_low)
    grad_value_w = dot_rows(attn_rows, value_grad_low)
    grad_attn_input = lax.psum_scatter(
        (
            dot_cols(query_grad, query_weight)
            + dot_cols(key_grad_low, key_weight)
            + dot_cols(value_grad_low, value_weight)
        ).astype(jnp.bfloat16),
        "tensor",
        scatter_dimension=0,
        tiled=True,
    ).astype(jnp.float32)
    grad_tokens = grad_mid + norm_back(grad_attn_input, normed_one, inverse_one, gain_one)
    gain_one_part = jnp.sum(grad_attn_input * normed_one, axis=0)
    gain_one_sum, gain_two_sum = lax.psum((gain_one_part, gain_two_part), "tensor")
    reduced = (
        lax.psum_scatter(
            gain_one_sum.astype(jnp.bfloat16), "dp", scatter_dimension=0, tiled=True
        ).astype(jnp.float32),
        lax.psum_scatter(
            gain_two_sum.astype(jnp.bfloat16), "dp", scatter_dimension=0, tiled=True
        ).astype(jnp.float32),
        lax.psum_scatter(
            grad_query_w.astype(jnp.bfloat16), "dp", scatter_dimension=0, tiled=True
        ).astype(jnp.float32),
        lax.psum_scatter(
            grad_key_w.astype(jnp.bfloat16), "dp", scatter_dimension=0, tiled=True
        ).astype(jnp.float32),
        lax.psum_scatter(
            grad_value_w.astype(jnp.bfloat16), "dp", scatter_dimension=0, tiled=True
        ).astype(jnp.float32),
        lax.psum_scatter(
            grad_out_w.astype(jnp.bfloat16), "dp", scatter_dimension=1, tiled=True
        ).astype(jnp.float32),
        lax.psum_scatter(
            grad_gate_w.astype(jnp.bfloat16), "dp", scatter_dimension=0, tiled=True
        ).astype(jnp.float32),
        lax.psum_scatter(
            grad_up_w.astype(jnp.bfloat16), "dp", scatter_dimension=0, tiled=True
        ).astype(jnp.float32),
        lax.psum_scatter(
            grad_down_w.astype(jnp.bfloat16), "dp", scatter_dimension=1, tiled=True
        ).astype(jnp.float32),
    )
    return (
        result,
        grad_tokens,
        reduced[0],
        reduced[1],
        reduced[2],
        reduced[3],
        reduced[4],
        reduced[5],
        reduced[6],
        reduced[7],
        reduced[8],
    )


def solution(mesh):
    return jax.shard_map(
        on_device,
        mesh=mesh,
        in_specs=(
            P(("dp", "tensor"), None),
            P(("dp", "tensor"), None),
            P("dp", None),
            P("dp"),
            P("dp"),
            P("dp", "tensor"),
            P("dp", "tensor"),
            P("dp", "tensor"),
            P("tensor", "dp"),
            P("dp", "tensor"),
            P("dp", "tensor"),
            P("tensor", "dp"),
        ),
        out_specs=(
            P(("dp", "tensor"), None),
            P(("dp", "tensor"), None),
            P("dp"),
            P("dp"),
            P("dp", "tensor"),
            P("dp", "tensor"),
            P("dp", "tensor"),
            P("tensor", "dp"),
            P("dp", "tensor"),
            P("dp", "tensor"),
            P("tensor", "dp"),
        ),
        check_vma=False,
    )
```

```python
import functools
import jax
import jax.numpy as jnp
from jax import lax
from jax.experimental import pallas as pl
from jax.experimental.pallas import tpu as pltpu
from jax.sharding import Mesh, PartitionSpec as P

QUERY_HEADS = 16
KEY_VALUE_HEADS = 8
HEAD_SIZE = 96
SEGS = 4
BF16 = jnp.bfloat16
F32 = jnp.float32
LOG2E = 1.4426950408889634
CHUNKS = 2

rope_base = 100000.0
small_eps = 1e-05
masked_value = -1e30


def dot_f32(left, right):
    return jnp.dot(left, right, preferred_element_type=F32)


def dot_rows(left, right):
    return lax.dot_general(left, right, (((0,), (0,)), ((), ())), preferred_element_type=F32)


def dot_cols(left, right):
    return lax.dot_general(left, right, (((1,), (1,)), ((), ())), preferred_element_type=F32)


def positions(segment_ids):
    labels = jnp.arange(SEGS, dtype=jnp.int32)
    member = (segment_ids[:, None] == labels).astype(jnp.int32)
    lengths_of = jnp.sum(member, axis=0)
    earlier = (labels < segment_ids[:, None]).astype(jnp.int32)
    first_row = jnp.sum(earlier * lengths_of[None, :], axis=-1)
    return jnp.arange(segment_ids.shape[0], dtype=jnp.int32) - first_row


def rms_scale(hidden):
    return lax.rsqrt(jnp.mean(hidden * hidden, axis=-1, keepdims=True) + small_eps)


def norm_back(grad_normed, normed, inverse, gain):
    scaled = grad_normed * gain
    return inverse * (scaled - normed * jnp.mean(scaled * normed, axis=-1, keepdims=True))


def rotate_turned(values, cosine, sine_table):
    half = HEAD_SIZE // 2
    front, back = values[:half], values[half:]
    return jnp.concatenate(
        [front * cosine - back * sine_table, back * cosine + front * sine_table], axis=0
    )


def project_kernel(
    index_ref, x_ref, gain_ref, w_ref, cos_ref, sin_ref, *refs, heads, chained
):
    a_ref, turned_ref = refs[-2:]
    hidden = x_ref[...].astype(F32)
    rows = (hidden * rms_scale(hidden) * gain_ref[...]).astype(BF16)
    a_ref[...] = rows
    turned = dot_f32(rows, w_ref[...]).T
    cosine, sine_table = cos_ref[...], sin_ref[...]
    pieces = [
        rotate_turned(turned[h * HEAD_SIZE : (h + 1) * HEAD_SIZE], cosine, sine_table)
        for h in range(heads)
    ]
    pieces.append(turned[heads * HEAD_SIZE :])
    turned_ref[...] = jnp.concatenate(pieces, axis=0).astype(BF16)


def project(index, x, gain, weights, width, heads, cosine, sine_table, total_rows, previous):
    rows, model = x.shape
    block = 256 if rows % 256 == 0 else 128
    steps = rows // block
    half = HEAD_SIZE // 2
    chained = previous is not None
    operands = [index, x, gain, weights, cosine, sine_table]
    in_specs = [
        pl.BlockSpec((block, model), lambda i, at: (i, 0)),
        pl.BlockSpec((1, model), lambda i, at: (0, 0)),
        pl.BlockSpec((model, width), lambda i, at: (0, 0)),
        pl.BlockSpec((half, block), lambda i, at: (0, at[0] * steps + i)),
        pl.BlockSpec((half, block), lambda i, at: (0, at[0] * steps + i)),
    ]
    aliases = {}
    if chained:
        operands += list(previous)
        in_specs += [pl.BlockSpec(memory_space=pl.ANY)] * 2
        aliases = {6: 0, 7: 1}
    return pl.pallas_call(
        functools.partial(project_kernel, heads=heads, chained=chained),
        grid_spec=pltpu.PrefetchScalarGridSpec(
            num_scalar_prefetch=1,
            grid=(steps,),
            in_specs=in_specs,
            out_specs=[
                pl.BlockSpec((block, model), lambda i, at: (at[0] * steps + i, 0)),
                pl.BlockSpec((width, block), lambda i, at: (0, at[0] * steps + i)),
            ],
        ),
        out_shape=[
            jax.ShapeDtypeStruct((total_rows, model), BF16),
            jax.ShapeDtypeStruct((width, total_rows), BF16),
        ],
        input_output_aliases=aliases,
        name="project",
    )(*operands)


def block_mask(kv_block, q_block, block, starts, diagonal):
    keys = kv_block * block + lax.broadcasted_iota(jnp.int32, (block, starts.shape[1]), 0)
    allowed = keys >= starts
    if diagonal:
        group = starts.shape[1] // block
        lanes = lax.broadcasted_iota(jnp.int32, (1, block), 1) + q_block * block
        allowed = allowed & (keys <= jnp.concatenate([lanes] * group, axis=1))
    return allowed


def forward_kernel(
    low_ref, high_ref, start_ref, qkv_ref, out_ref, lse_ref, k_ref, vt_ref, acc_ref,
    *, heads, kv_heads, block, scale,
):
    step = pl.program_id(0)
    rows = qkv_ref.shape[1]
    group = heads // kv_heads
    factor = scale * LOG2E
    q_width = heads * HEAD_SIZE
    k_width = kv_heads * HEAD_SIZE

    @pl.when(step == 0)
    def _():
        @pl.loop(0, rows // block)
        def _(at):
            here = pl.ds(pl.multiple_of(at * block, block), block)
            for kv in range(kv_heads):
                begin = q_width + kv * HEAD_SIZE
                k_ref[kv, here, :] = qkv_ref[begin : begin + HEAD_SIZE, here].T
                begin = begin + k_width
                vt_ref[kv, :HEAD_SIZE, here] = qkv_ref[begin : begin + HEAD_SIZE, here]
                vt_ref[kv, HEAD_SIZE:, here] = jnp.ones((16, block), BF16)

    here = pl.ds(pl.multiple_of(step * block, block), block)
    starts = jnp.concatenate([start_ref[:, here]] * group, axis=1)
    turned_queries = [
        jnp.concatenate(
            [
                qkv_ref[(kv * group + g) * HEAD_SIZE : (kv * group + g + 1) * HEAD_SIZE, here]
                for g in range(group)
            ],
            axis=1,
        )
        for kv in range(kv_heads)
    ]

    def scores(kv, kv_block, masked, diagonal):
        there = pl.ds(pl.multiple_of(kv_block * block, block), block)
        raw = dot_f32(k_ref[kv, there, :], turned_queries[kv])
        if masked:
            raw = jnp.where(
                block_mask(kv_block, step, block, starts, diagonal), raw, masked_value
            )
        return raw

    def attend(kv, kv_block, probs):
        there = pl.ds(pl.multiple_of(kv_block * block, block), block)
        return dot_f32(vt_ref[kv, :, there], probs.astype(BF16))

    largest = []
    for kv in range(kv_heads):
        raw = scores(kv, step, True, True)
        top = jnp.max(raw, axis=0, keepdims=True)
        acc_ref[kv] = attend(kv, step, jnp.exp2((raw - top) * factor))
        largest.append(top)

    def more(masked):
        def body(kv_block, tops):
            result = []
            for kv in range(kv_heads):
                raw = scores(kv, kv_block, masked, False)
                top = jnp.maximum(tops[kv], jnp.max(raw, axis=0, keepdims=True))
                shrink = jnp.exp2((tops[kv] - top) * factor)
                acc_ref[kv] = acc_ref[kv] * shrink + attend(
                    kv, kv_block, jnp.exp2((raw - top) * factor)
                )
                result.append(top)
            return tuple(result)

        return body

    low = low_ref[step]
    high = jnp.minimum(high_ref[step], step)
    tops = lax.fori_loop(low, high, more(True), tuple(largest))
    tops = lax.fori_loop(jnp.maximum(low, high), step, more(False), tops)
    outs = []
    for kv in range(kv_heads):
        total = acc_ref[kv, HEAD_SIZE : HEAD_SIZE + 1, :]
        result = (acc_ref[kv, :HEAD_SIZE, :] / total).astype(BF16)
        logs = tops[kv] * factor + jnp.log2(total)
        for g in range(group):
            outs.append(result[:, g * block : (g + 1) * block])
            lse_ref[kv * group + g : kv * group + g + 1, :] = logs[:, g * block : (g + 1) * block]
    out_ref[...] = jnp.concatenate(outs, axis=0).T


def attention_forward(qkv, starts, low, high, heads, kv_heads, block):
    width, rows = qkv.shape
    q_width = heads * HEAD_SIZE
    group = heads // kv_heads
    return pl.pallas_call(
        functools.partial(
            forward_kernel, heads=heads, kv_heads=kv_heads, block=block, scale=HEAD_SIZE**-0.5
        ),
        grid_spec=pltpu.PrefetchScalarGridSpec(
            num_scalar_prefetch=2,
            grid=(rows // block,),
            in_specs=[
                pl.BlockSpec((1, rows), lambda i, *_: (0, 0)),
                pl.BlockSpec((width, rows), lambda i, *_: (0, 0)),
            ],
            out_specs=[
                pl.BlockSpec((block, q_width), lambda i, *_: (i, 0)),
                pl.BlockSpec((heads, block), lambda i, *_: (0, i)),
            ],
            scratch_shapes=[
                pltpu.VMEM((kv_heads, rows, HEAD_SIZE), BF16),
                pltpu.VMEM((kv_heads, HEAD_SIZE + 16, rows), BF16),
                pltpu.VMEM((kv_heads, HEAD_SIZE + 16, group * block), F32),
            ],
        ),
        out_shape=[
            jax.ShapeDtypeStruct((rows, q_width), BF16),
            jax.ShapeDtypeStruct((heads, rows), F32),
        ],
        name="attention_forward",
    )(low, high, starts, qkv)


def unrotate_turned(values, cosine, sine_table):
    half = HEAD_SIZE // 2
    front, back = values[:half], values[half:]
    return jnp.concatenate(
        [front * cosine + back * sine_table, back * cosine - front * sine_table], axis=0
    )


def backward_kernel(
    low_ref, high_ref, start_ref, qkv_ref, out_ref, grad_ref, lse_ref, cos_ref, sin_ref,
    result_ref, k_ref, v_ref, dk_ref, dv_ref, dq_ref, turned_ref,
    *, heads, kv_heads, block, scale,
):
    step = pl.program_id(0)
    rows = qkv_ref.shape[1]
    group = heads // kv_heads
    factor = scale * LOG2E
    q_width = heads * HEAD_SIZE
    k_width = kv_heads * HEAD_SIZE

    @pl.when(step == 0)
    def _():
        dk_ref[...] = jnp.zeros_like(dk_ref)
        dv_ref[...] = jnp.zeros_like(dv_ref)

        @pl.loop(0, rows // block)
        def _(at):
            here = pl.ds(pl.multiple_of(at * block, block), block)
            for kv in range(kv_heads):
                begin = q_width + kv * HEAD_SIZE
                k_ref[kv, here, :] = qkv_ref[begin : begin + HEAD_SIZE, here].T
                begin = begin + k_width
                v_ref[kv, here, :] = qkv_ref[begin : begin + HEAD_SIZE, here].T

    here = pl.ds(pl.multiple_of(step * block, block), block)
    starts = jnp.concatenate([start_ref[:, here]] * group, axis=1)
    turned_q = qkv_ref[:q_width, here]
    turned_grad = grad_ref[...].T
    turned_out = out_ref[...].T
    product = turned_grad.astype(F32) * turned_out.astype(F32)
    queries, queries_turned, grads, grads_turned, inners, logs = [], [], [], [], [], []
    for kv in range(kv_heads):
        pieces = [
            (slice((kv * group + g) * HEAD_SIZE, (kv * group + g + 1) * HEAD_SIZE))
            for g in range(group)
        ]
        queries_turned.append(jnp.concatenate([turned_q[s] for s in pieces], axis=1))
        grads_turned.append(jnp.concatenate([turned_grad[s] for s in pieces], axis=1))
        queries.append(jnp.concatenate([turned_q[s].T for s in pieces], axis=0))
        grads.append(jnp.concatenate([turned_grad[s].T for s in pieces], axis=0))
        inners.append(
            jnp.concatenate([jnp.sum(product[s], axis=0, keepdims=True) for s in pieces], axis=1)
        )
        logs.append(
            jnp.concatenate(
                [lse_ref[kv * group + g : kv * group + g + 1, :] for g in range(group)], axis=1
            )
        )

    def block_step(kv_block, masked, diagonal):
        there = pl.ds(pl.multiple_of(kv_block * block, block), block)
        if masked:
            allowed = block_mask(kv_block, step, block, starts, diagonal)
        for kv in range(kv_heads):
            raw = dot_f32(k_ref[kv, there, :], queries_turned[kv])
            if masked:
                raw = jnp.where(allowed, raw, masked_value)
            probs = jnp.exp2(raw * factor - logs[kv])
            grad_soft = dot_f32(v_ref[kv, there, :], grads_turned[kv])
            grad_raw = (probs * (grad_soft - inners[kv])).astype(BF16)
            dv_ref[kv, there, :] += dot_f32(probs.astype(BF16), grads[kv])
            dk_ref[kv, there, :] += dot_f32(grad_raw, queries[kv])
            k_begin = q_width + kv * HEAD_SIZE
            dq = dot_f32(qkv_ref[k_begin : k_begin + HEAD_SIZE, there], grad_raw)
            if diagonal:
                dq_ref[kv] = dq
            else:
                dq_ref[kv] += dq

    block_step(step, True, True)
    low = low_ref[step]
    high = jnp.minimum(high_ref[step], step)

    @pl.loop(low, high)
    def _(kv_block):
        block_step(kv_block, True, False)

    @pl.loop(jnp.maximum(low, high), step)
    def _(kv_block):
        block_step(kv_block, False, False)

    cosine, sine_table = cos_ref[:, here], sin_ref[:, here]
    for kv in range(kv_heads):
        for g in range(group):
            head = kv * group + g
            turned = dq_ref[kv, :, g * block : (g + 1) * block] * scale
            turned_ref[head * HEAD_SIZE : (head + 1) * HEAD_SIZE, here] = unrotate_turned(
                turned, cosine, sine_table
            ).astype(BF16)

    @pl.when(step == pl.num_programs(0) - 1)
    def _():
        @pl.loop(0, rows // block)
        def _(at):
            here = pl.ds(pl.multiple_of(at * block, block), block)
            pieces = [turned_ref[:, here]]
            for kv in range(kv_heads):
                turned = dk_ref[kv, here, :].T * scale
                pieces.append(
                    unrotate_turned(turned, cos_ref[:, here], sin_ref[:, here]).astype(
                        BF16
                    )
                )
            for kv in range(kv_heads):
                pieces.append(dv_ref[kv, here, :].T.astype(BF16))
            result_ref[here, :] = jnp.concatenate(pieces, axis=0).T


def attention_backward(
    qkv, out, grad, logs, starts, low, high, cosine, sine_table, heads, kv_heads, block
):
    width, rows = qkv.shape
    q_width = heads * HEAD_SIZE
    group = heads // kv_heads
    half = HEAD_SIZE // 2
    whole = lambda i, *_: (0, 0)
    return pl.pallas_call(
        functools.partial(
            backward_kernel, heads=heads, kv_heads=kv_heads, block=block, scale=HEAD_SIZE**-0.5
        ),
        grid_spec=pltpu.PrefetchScalarGridSpec(
            num_scalar_prefetch=2,
            grid=(rows // block,),
            in_specs=[
                pl.BlockSpec((1, rows), whole),
                pl.BlockSpec((width, rows), whole),
                pl.BlockSpec((block, q_width), lambda i, *_: (i, 0)),
                pl.BlockSpec((block, q_width), lambda i, *_: (i, 0)),
                pl.BlockSpec((heads, block), lambda i, *_: (0, i)),
                pl.BlockSpec((half, rows), whole),
                pl.BlockSpec((half, rows), whole),
            ],
            out_specs=pl.BlockSpec((rows, width), whole),
            scratch_shapes=[
                pltpu.VMEM((kv_heads, rows, HEAD_SIZE), BF16),
                pltpu.VMEM((kv_heads, rows, HEAD_SIZE), BF16),
                pltpu.VMEM((kv_heads, rows, HEAD_SIZE), F32),
                pltpu.VMEM((kv_heads, rows, HEAD_SIZE), F32),
                pltpu.VMEM((kv_heads, HEAD_SIZE, group * block), F32),
                pltpu.VMEM((q_width, rows), BF16),
            ],
        ),
        out_shape=jax.ShapeDtypeStruct((rows, width), BF16),
        name="attention_backward",
    )(low, high, starts, qkv, out, grad, logs, cosine, sine_table)


def block_bounds(starts, block):
    firsts = starts[0, ::block]
    lasts = starts[0, block - 1 :: block]
    return firsts // block, (lasts + block - 1) // block


def units_kernel(a_ref, c_ref, w_ref, hid_ref, gu_ref, dw_ref, acc_ref, *, width):
    step = pl.program_id(0)
    a, c = a_ref[...], c_ref[...]
    gate = dot_f32(a, w_ref[:, :width])
    up = dot_f32(a, w_ref[:, width : 2 * width])
    grad = dot_f32(c, w_ref[:, 2 * width :])
    sigmoid = 1.0 / (1.0 + jnp.exp(-gate))
    act = gate * sigmoid
    hid = (act * up).astype(BF16)
    dg = (grad * up * sigmoid * (1.0 + gate * (1.0 - sigmoid))).astype(BF16)
    du = (grad * act).astype(BF16)
    hid_ref[...] = hid
    gu = jnp.concatenate([dg, du], axis=1)
    gu_ref[...] = gu
    dw_gu = dot_rows(a, gu)
    dw_d = dot_rows(c, hid)
    last = pl.num_programs(0) - 1

    @pl.when(step == 0)
    def _():
        acc_ref[:, : 2 * width] = dw_gu
        acc_ref[:, 2 * width :] = dw_d

    @pl.when((step > 0) & (step < last))
    def _():
        acc_ref[:, : 2 * width] += dw_gu
        acc_ref[:, 2 * width :] += dw_d

    @pl.when(step == last)
    def _():
        dw_ref[:, : 2 * width] = (acc_ref[:, : 2 * width] + dw_gu).astype(BF16)
        dw_ref[:, 2 * width :] = (acc_ref[:, 2 * width :] + dw_d).astype(BF16)


def units(a, c, w, rows_block):
    rows, model = a.shape
    width = w.shape[1] // 3
    row_spec = pl.BlockSpec((rows_block, model), lambda i: (i, 0))
    whole = pl.BlockSpec(w.shape, lambda i: (0, 0))
    return pl.pallas_call(
        functools.partial(units_kernel, width=width),
        grid=(rows // rows_block,),
        in_specs=[row_spec, row_spec, whole],
        out_specs=[
            pl.BlockSpec((rows_block, width), lambda i: (i, 0)),
            pl.BlockSpec((rows_block, 2 * width), lambda i: (i, 0)),
            whole,
        ],
        out_shape=[
            jax.ShapeDtypeStruct((rows, width), BF16),
            jax.ShapeDtypeStruct((rows, 2 * width), BF16),
            jax.ShapeDtypeStruct(w.shape, BF16),
        ],
        scratch_shapes=[pltpu.VMEM(w.shape, F32)],
        name="units",
    )(a, c, w)


def sum_kernel(*refs, count):
    total = dot_cols(refs[0][...], refs[count][...])
    for at in range(1, count):
        total += dot_cols(refs[at][...], refs[count + at][...])
    refs[-1][...] = total.astype(refs[-1].dtype)


def sum_products(lefts, rights, begin, rows, first, part, dtype, rows_block):
    model = rights[0].shape[0]
    depth = lefts[0].shape[1]
    offset = begin // rows_block
    return pl.pallas_call(
        functools.partial(sum_kernel, count=len(lefts)),
        grid=(rows // rows_block,),
        in_specs=[pl.BlockSpec((rows_block, depth), lambda i: (i + offset, 0)) for _ in lefts]
        + [
            pl.BlockSpec((model, depth), lambda i: (0, part), pipeline_mode=pl.Buffered(1))
            for _ in rights
        ],
        out_specs=pl.BlockSpec((rows_block, model), lambda i: (i, 0)),
        out_shape=jax.ShapeDtypeStruct((rows, model), dtype),
        name="sum_products",
    )(*lefts, *rights)


def on_device(
    tokens,
    cotangent,
    seg_ids,
    gain_attn,
    gain_ffn,
    w_query,
    w_key,
    value_projection,
    w_out,
    w_gate,
    w_up,
    w_down,
    *,
    planes,
    lanes,
):
    core = lax.axis_index("core")
    place = lax.axis_index("tensor")
    first_core = core == 0
    phases = lanes.bit_length() - 1
    bits = [1 << k for k in range(phases)]
    orders = (bits, bits[::-1])
    tables = [
        [sum(order[k] for k in range(phases) if slot >> k & 1) for slot in range(lanes)]
        for order in orders
    ]
    mirror = [tables[1].index(offset) for offset in tables[0]]
    natural = [
        place ^ jnp.where(first_core, tables[0][slot], tables[1][slot]) for slot in range(lanes)
    ]

    def swap(value):
        return lax.ppermute(value, "core", [(0, 1), (1, 0)])

    def exchange(value, offsets):
        pairs = [
            (c * lanes + i, c * lanes + (i ^ offsets[c])) for c in range(2) for i in range(lanes)
        ]
        return lax.ppermute(value, ("core", "tensor"), pairs)

    def hop(value, phase):
        return exchange(value, [order[phase] for order in orders])

    def to_slot(value, slot):
        if slot == 0:
            return value
        return exchange(value, [table[slot] for table in tables])

    def spread(value):
        have = [value]
        for phase in range(phases):
            have = have + [hop(v, phase) for v in have]
        return have

    def collect(slots):
        have = list(slots)
        for phase in reversed(range(phases)):
            half = 1 << phase
            arrived = [hop(have[half + at], phase) for at in range(half)]
            have = [
                have[at].astype(F32) + arrived[at].astype(F32) for at in range(half)
            ]
            if phase > 0:
                have = [v.astype(BF16) for v in have]
        return have[0]

    def mine(value, axis):
        return lax.dynamic_index_in_dim(value, core, axis, keepdims=False)

    def theirs(value, axis):
        return lax.dynamic_index_in_dim(value, 1 - core, axis, keepdims=False)

    def by_core(own, other):
        return jnp.where(first_core, own, other), jnp.where(first_core, other, own)

    rows, model = tokens.shape
    shard = w_query.shape[0]
    pack_rows = seg_ids.shape[1]
    q_width = w_query.shape[1]
    k_width = w_key.shape[1]
    width = q_width + 2 * k_width
    heads = q_width // HEAD_SIZE
    kv_heads = k_width // HEAD_SIZE

    token_slots = spread(tokens)
    gains = jnp.pad(jnp.stack([gain_attn, gain_ffn], axis=1), ((0, 0), (0, 126)))
    attn_weights = lax.all_gather(
        jnp.concatenate([w_query, w_key, value_projection, w_out.T, gains], axis=1),
        ("z", "core"),
        axis=0,
        tiled=True,
    )
    cotangent_pair = jnp.concatenate([cotangent, swap(cotangent)], axis=0)
    units_local = w_gate.shape[1]
    part = units_local // (2 * CHUNKS)
    stacked = jnp.stack([w_gate, w_up, w_down.T], axis=1).reshape(shard, 3, 2, CHUNKS, part)
    kept = mine(stacked, 2)
    arrived = swap(theirs(stacked, 2))
    unit_weights = []
    for chunk in range(CHUNKS):
        low_rows, high_rows = by_core(
            kept[:, :, chunk].reshape(shard, 3 * part),
            arrived[:, :, chunk].reshape(shard, 3 * part),
        )
        gathered = lax.all_gather(
            jnp.concatenate([low_rows, high_rows], axis=0), "z", axis=0, tiled=True
        )
        unit_weights.append(spread(gathered))

    gain_rows = attn_weights[:, width + q_width : width + q_width + 2].astype(F32).T
    gain_one, gain_two = gain_rows[0:1], gain_rows[1:2]
    out_own = attn_weights[:, width : width + q_width].reshape(planes, 2, shard, q_width)
    out_mine = spread(mine(out_own, 1).reshape(planes * shard, q_width))
    out_theirs = [theirs(out_own, 1).reshape(planes * shard, q_width)] + [
        swap(out_mine[mirror[slot]]) for slot in range(1, lanes)
    ]
    out_weights = []
    for own, other in zip(out_mine, out_theirs):
        low_rows, high_rows = by_core(own, other)
        out_weights.append(
            jnp.stack(
                [
                    low_rows.reshape(planes, shard, q_width),
                    high_rows.reshape(planes, shard, q_width),
                ],
                axis=1,
            ).reshape(model, q_width)
        )
    out_weights = jnp.concatenate(out_weights, axis=1)

    segment_row = seg_ids[0]
    position_ids = positions(segment_row)
    frequency = rope_base ** (-jnp.arange(HEAD_SIZE // 2, dtype=F32) * 2.0 / HEAD_SIZE)
    phase_angle = position_ids.astype(F32)[None, :] * frequency[:, None]
    cosine, sine_table = jnp.cos(phase_angle), jnp.sin(phase_angle)
    starts = (jnp.arange(pack_rows, dtype=jnp.int32) - position_ids)[None, :]
    low_512, high_512 = block_bounds(starts, 512)
    low_256, high_256 = block_bounds(starts, 256)
    projected = None
    for slot in range(lanes):
        projected = project(
            natural[slot][None].astype(jnp.int32),
            token_slots[slot],
            gain_one,
            attn_weights,
            width,
            heads + kv_heads,
            cosine,
            sine_table,
            pack_rows,
            projected,
        )
    attn_rows, qkv = projected
    attn_out, log_totals = attention_forward(
        qkv, starts, low_512, high_512, heads, kv_heads, 512
    )
    out_slots = [
        to_slot(lax.dynamic_slice_in_dim(attn_out, natural[slot] * rows, rows, 0), slot)
        for slot in range(lanes)
    ]
    out_rows = jnp.concatenate(out_slots, axis=1)
    hidden_in = tokens.astype(F32)
    inverse_one = rms_scale(hidden_in)
    normed_one = hidden_in * inverse_one
    hidden_mid = hidden_in + dot_cols(out_rows, out_weights)
    inverse_two = rms_scale(hidden_mid)
    normed_two = hidden_mid * inverse_two
    ffn_input = (normed_two * gain_two).astype(BF16)
    ffn_pair = jnp.concatenate([ffn_input, swap(ffn_input)], axis=0)

    unit_rows = 768 if (2 * rows) % 768 == 0 else 2 * rows
    hids, grads, unit_grads = [], [], [[] for _ in range(CHUNKS)]
    weights_used = []
    for slot in range(lanes):
        for chunk in range(CHUNKS):
            weight = unit_weights[chunk][slot]
            hid, grad, grad_w = units(ffn_pair, cotangent_pair, weight, unit_rows)
            hids.append(hid)
            grads.append(grad)
            weights_used.append(weight)
            unit_grads[chunk].append(grad_w)
    sum_rows = 256 if rows % 256 == 0 else 128
    their_grad = swap(
        sum_products(grads, weights_used, rows, rows, 0, 0, F32, sum_rows)
    )
    my_grad = sum_products(grads, weights_used, 0, rows, 0, 0, F32, sum_rows)
    grad_ffn_input = my_grad + their_grad
    their_sum = swap(sum_products(hids, weights_used, rows, rows, 0, 2, BF16, sum_rows))
    my_sum = sum_products(hids, weights_used, 0, rows, 0, 2, F32, sum_rows)
    result = (hidden_mid + (my_sum + their_sum.astype(F32))).astype(BF16)

    grad_mid = cotangent.astype(F32) + norm_back(
        grad_ffn_input, normed_two, inverse_two, gain_two
    )
    gain_two_part = jnp.sum(grad_ffn_input * normed_two, axis=0)
    grad_branch = grad_mid.astype(BF16)

    grad_out_rows = dot_f32(grad_branch, out_weights).astype(BF16)
    grad_attended = jnp.zeros((pack_rows, q_width), BF16)
    for slot in range(lanes):
        piece = to_slot(grad_out_rows[:, slot * q_width : (slot + 1) * q_width], slot)
        grad_attended = lax.dynamic_update_slice_in_dim(
            grad_attended, piece, natural[slot] * rows, 0
        )
    grad_out_w = (
        dot_rows(grad_branch, out_rows).astype(BF16).reshape(planes, 2, shard, lanes, q_width)
    )
    sent = theirs(grad_out_w, 1)
    sent = swap(jnp.stack([sent[:, :, mirror[slot]] for slot in range(lanes)], axis=2))
    grad_out_w = (mine(grad_out_w, 1).astype(F32) + sent.astype(F32)).astype(BF16)
    grad_out_w = collect(
        [grad_out_w[:, :, slot].reshape(planes * shard, q_width) for slot in range(lanes)]
    )
    grad_out_w = lax.psum_scatter(
        grad_out_w.astype(BF16), "z", scatter_dimension=0, tiled=True
    )
    grad_qkv = attention_backward(
        qkv,
        attn_out,
        grad_attended,
        log_totals,
        starts,
        low_256,
        high_256,
        cosine,
        sine_table,
        heads,
        kv_heads,
        256,
    )
    projection = attn_weights[:, :width]
    grad_slots = [
        dot_cols(
            lax.dynamic_slice_in_dim(grad_qkv, natural[slot] * rows, rows, 0), projection
        ).astype(BF16)
        for slot in range(lanes)
    ]
    grad_attn_input = collect(grad_slots)
    grad_qkv_w = lax.psum_scatter(
        dot_rows(attn_rows, grad_qkv).astype(BF16),
        ("z", "core"),
        scatter_dimension=0,
        tiled=True,
    ).astype(F32)
    grad_tokens = grad_mid + norm_back(grad_attn_input, normed_one, inverse_one, gain_one)
    gain_one_part = jnp.sum(grad_attn_input * normed_one, axis=0)

    unit_pieces = []
    for chunk in range(CHUNKS):
        summed = collect(unit_grads[chunk]).astype(BF16)
        scattered = lax.psum_scatter(summed, "z", scatter_dimension=0, tiled=True)
        scattered = scattered.reshape(2, shard, 3, part)
        low_part, high_part = by_core(mine(scattered, 0), swap(theirs(scattered, 0)))
        unit_pieces.append((low_part, high_part))
    unit_w = jnp.concatenate(
        [piece[0] for piece in unit_pieces] + [piece[1] for piece in unit_pieces], axis=2
    ).astype(F32)
    gain_sums = lax.psum(
        jnp.stack([gain_one_part, gain_two_part]), ("z", "core", "tensor")
    )
    owner = lax.axis_index("z") * 2 + core
    gain_sums = lax.dynamic_slice_in_dim(gain_sums, owner * shard, shard, 1)
    return (
        result,
        grad_tokens,
        gain_sums[0],
        gain_sums[1],
        grad_qkv_w[:, :q_width],
        grad_qkv_w[:, q_width : q_width + k_width],
        grad_qkv_w[:, q_width + k_width :],
        grad_out_w.astype(F32).T,
        unit_w[:, 0],
        unit_w[:, 1],
        unit_w[:, 2].T,
    )


def solution(mesh):
    packs, lanes = mesh.shape["dp"], mesh.shape["tensor"]
    split_mesh = Mesh(mesh.devices.reshape(packs // 2, 2, lanes), ("z", "core", "tensor"))
    dp = ("z", "core")
    everywhere = ("z", "core", "tensor")
    return jax.shard_map(
        functools.partial(on_device, planes=packs // 2, lanes=lanes),
        mesh=split_mesh,
        in_specs=(
            P(everywhere, None),
            P(everywhere, None),
            P(dp, None),
            P(dp),
            P(dp),
            P(dp, "tensor"),
            P(dp, "tensor"),
            P(dp, "tensor"),
            P("tensor", dp),
            P(dp, "tensor"),
            P(dp, "tensor"),
            P("tensor", dp),
        ),
        out_specs=(
            P(everywhere, None),
            P(everywhere, None),
            P(dp),
            P(dp),
            P(dp, "tensor"),
            P(dp, "tensor"),
            P(dp, "tensor"),
            P("tensor", dp),
            P(dp, "tensor"),
            P(dp, "tensor"),
            P("tensor", dp),
        ),
        check_vma=False,
    )
```
